512 devices in a mesh: seq: 64 (over y, x, z_lo), tp: 8 (over z_hi, core).
Axes of the slice: x: 4, y: 4, z: 16 (z_hi: 4, z_lo: 4; z = z_hi * 4 + z_lo), core: 2. Of those that a mesh axis runs over, the one named last changes fastest.
Arguments:
- q_feat: bfloat16 [16384, 4096], P('seq', 'tp'), may hold values from -6 to 6
- k_feat: bfloat16 [16384, 4096], P('seq', 'tp'), may hold values from -6 to 6
- v_feat: bfloat16 [16384, 4096], P('seq', 'tp'), may hold values from -6 to 6
- stream: bfloat16 [16384, 4096], P('seq', 'tp'), may hold values from -6 to 6
- filters: float32 [4096, 16384], P(('tp', 'seq')), may hold values from -1.2 to 1.2
- w_out: bfloat16 [4096, 4096], P('tp', 'seq'), may hold values from -0.25 to 0.25
Outputs:
- mixed_out: bfloat16 [16384, 4096], P('seq', 'tp')
The draws below stay inside these ranges and needn't reach their ends.
All inputs are finite; a program needn't handle non-finite values.
Results may differ from the reference program's by a relative error of at most 0.012.
Values may be sent and summed in bfloat16 or wider, within the bound.
No kernel may reach another device: no remote copies, remote signals or barrier semaphores. Data moves between devices by JAX's collectives and lax.ppermute only.
A program may use at most 64 MiB of HBM per device.

```python
import math
import jax
import jax.numpy as jnp
from jax import lax

D = 4096
L = 16384


def draw_filters(key, part):
    keys = jax.random.split(jax.random.fold_in(key, 71), 6)
    segment_starts = jnp.arange(L, dtype=jnp.float32)
    spans = jnp.exp(jax.random.uniform(keys[0], (D,), jnp.float32, math.log(30.0), math.log(64.0 * L)))
    amplitude = jnp.sqrt(1.0 - jnp.exp(-2.0 / spans))
    noise = jax.random.truncated_normal(keys[3], -4.0, 4.0, (D, L), jnp.float32)
    sequence_indices = jax.random.randint(keys[4], (D, 4), 0, L)
    discarded_entries = jax.random.uniform(keys[5], (D, 4), jnp.float32, 0.5, 0.8)
    normalizing_multiplier = jnp.ones((D, L), jnp.float32)
    for kernel_tap_group in range(4):
        normalizing_multiplier = normalizing_multiplier * jnp.where(segment_starts[None, :] >= sequence_indices[:, kernel_tap_group:kernel_tap_group + 1].astype(jnp.float32), discarded_entries[:, kernel_tap_group:kernel_tap_group + 1], 1.0)
    base = amplitude[:, None] * jnp.exp(-segment_starts[None, :] / spans[:, None]) * normalizing_multiplier
    return base * noise


def raised(values, own_key, source, target, parts, factor):
    def block_of(position):
        return (jnp.arange(values.shape[position]) // (values.shape[position] // parts)).reshape((-1,) + (1,) * (values.ndim - 1 - position))

    near = jax.random.permutation(own_key, parts)[block_of(target)]
    other_side = (block_of(target) + parts // 2) % parts
    return jnp.where((block_of(source) == near) | (block_of(source) == other_side), factor * values, values)


def block_levels(own_key, shape, cuts, least, top_value):
    def one(dim, shards_of):
        steps = jax.random.uniform(jax.random.fold_in(jax.random.fold_in(own_key, 6), dim), (shards_of,), jnp.float32, least / len(cuts), top_value / len(cuts))
        return jnp.repeat(jnp.exp(steps), shape[dim] // shards_of).reshape((-1,) + (1,) * (len(shape) - dim - 1))

    level = one(*cuts[0])
    for cut in cuts[1:]:
        level = level * one(*cut)
    return level


def scatter_about(stream_key, extent, deviation, reach, shards=(), held_as=jnp.bfloat16):
    entries = deviation * jax.random.normal(stream_key, extent, jnp.float32)
    if shards:
        entries = entries * block_levels(stream_key, extent, shards, -0.22, 0.18)
    return jnp.clip(entries, -reach, reach).astype(held_as)


def bell_draw_with(stream_key, dims, width, most, shards, heavy, kind=jnp.bfloat16):
    array = width * jax.random.normal(stream_key, dims, jnp.float32)
    if shards:
        array = array * block_levels(stream_key, dims, shards, -0.22, 0.18)
    return jnp.clip(raised(array, jax.random.fold_in(stream_key, 3), *heavy), -most, most).astype(kind)


def setup_inputs(seed: int = 0) -> dict:
    splits = jax.random.split(jax.random.key(seed), 7)
    q_feat = scatter_about(splits[0], (L, D), 1.0, 6.0, ((0, 64), (1, 8)))
    k_feat = scatter_about(splits[1], (L, D), 1.0, 6.0, ((0, 64), (1, 8)))
    v_feat = scatter_about(splits[2], (L, D), 1.0, 6.0, ((0, 64), (1, 8)))
    stream = scatter_about(splits[3], (L, D), 1.0, 6.0, ((0, 64), (1, 8)))
    filters = draw_filters(jax.random.fold_in(splits[6], 71), 0)
    w_out = bell_draw_with(splits[5], (D, D), D ** -0.5, 0.25, ((0, 8), (1, 64)), (0, 1, 64, 4.0))
    return dict(q_feat=q_feat, k_feat=k_feat, v_feat=v_feat, stream=stream, filters=filters, w_out=w_out)


def convolve_block(pair):
    signal, taps = pair
    length = signal.shape[1]
    spectrum = jnp.fft.rfft(signal, n=2 * length, axis=1) * jnp.fft.rfft(taps, n=2 * length, axis=1)
    return jnp.fft.irfft(spectrum, n=2 * length, axis=1)[:, :length]


def reference(q_feat, k_feat, v_feat, stream, filters, w_out):
    mixed = (k_feat.astype(jnp.float32) * v_feat.astype(jnp.float32)).astype(jnp.bfloat16)
    blocksize = math.gcd(D, 256)
    signal = mixed.astype(jnp.float32).T.reshape(D // blocksize, blocksize, L)
    taps = filters.astype(jnp.float32).reshape(D // blocksize, blocksize, L)
    conv = lax.map(convolve_block, (signal, taps)).reshape(D, L).T
    conv = lax.optimization_barrier(conv.astype(jnp.float32).astype(jnp.bfloat16))
    gated = (q_feat.astype(jnp.float32) * conv.astype(jnp.float32)).astype(jnp.bfloat16)
    projected = jnp.dot(gated, w_out, preferred_element_type=jnp.float32)
    return (stream.astype(jnp.float32) + projected).astype(jnp.bfloat16)
```

```python
import functools

import jax
import jax.numpy as jnp
import numpy as np
from jax import lax
from jax.experimental import pallas as pl
from jax.experimental.pallas import tpu as pltpu
from jax.sharding import Mesh
from jax.sharding import PartitionSpec as P

SEQ = ("y", "x", "zl")
ALL = ("y", "x", "zl", "zh", "c")
B = 256
N = 64
TOP = B * (N - 1) + 128
ROWS = TOP + B


def build_bank(h_ref, c, bank):
    lane = lax.broadcasted_iota(jnp.int32, (16, 128), 1)
    row = lax.broadcasted_iota(jnp.int32, (16, 128), 0)
    low = lane < row
    zero = jnp.zeros((16, 128), jnp.bfloat16)

    def put(w, val):
        v = TOP // 16 - w
        if 0 <= v < ROWS // 16:
            bank[pl.ds(16 * v, 16), :] = val

    rolled_before = jnp.zeros((16, 128), jnp.float32)
    before = zero
    for w in range(-16, -8):
        put(w, zero)
    for m in range(128):
        taps = jnp.broadcast_to(h_ref[c, pl.ds(m, 1), :], (16, 128))
        rolled = pltpu.roll(taps, 0, 1, stride=1, stride_axis=0)
        here = jnp.where(low, rolled_before, rolled).astype(jnp.bfloat16)
        rolled_before = rolled
        for j in range(1, 8):
            put(8 * (m - 1) + j, jnp.concatenate([before[:, 16 * j :], here[:, : 16 * j]], axis=1))
        put(8 * m, here)
        before = here


def conv_body(x_ref, h_ref, o_ref, padded, bank, acc0, acc1):
    padded[pl.ds(0, N), :] = jnp.zeros((N, B), jnp.float32)

    def channel(c, carry):
        padded[pl.ds(N, N), :] = x_ref[c].astype(jnp.float32)
        build_bank(h_ref, c, bank)
        for k in range(N):
            mxu, stage = k % 2, (k // 2) % 2
            r0 = TOP - B * k
            rhs = jnp.concatenate([bank[pl.ds(r0, B), :], bank[pl.ds(r0 - 128, B), :]], axis=1)
            pltpu.matmul_push_rhs(rhs, stage, mxu)
            lhs = padded[pl.ds(N - k, N), :].astype(jnp.bfloat16)
            pltpu.matmul_acc_lhs((acc0, acc1)[mxu], lhs, load_staged_rhs=stage)
        o_ref[c] = (pltpu.matmul_pop(acc0) + pltpu.matmul_pop(acc1)).astype(jnp.bfloat16)
        return carry

    lax.fori_loop(0, 8, channel, 0)


def conv_kernel(*refs):
    pl.run_scoped(
        functools.partial(conv_body, *refs),
        pltpu.ACC(0)((N, B), jnp.float32),
        pltpu.ACC(1)((N, B), jnp.float32),
    )


def causal_conv(x, taps):
    return pl.pallas_call(
        conv_kernel,
        out_shape=jax.ShapeDtypeStruct((8, N, B), jnp.bfloat16),
        in_specs=[pl.BlockSpec(memory_space=pltpu.VMEM)] * 2,
        out_specs=pl.BlockSpec(memory_space=pltpu.VMEM),
        scratch_shapes=[
            pltpu.VMEM((2 * N, B), jnp.float32),
            pltpu.VMEM((ROWS, 128), jnp.bfloat16),
        ],
        cost_estimate=pl.CostEstimate(flops=2**32, bytes_accessed=2**20, transcendentals=0),
        name="causal_conv",
    )(x, taps.reshape(8, 128, 128))


def place(y, x, zl, zh, c):
    return (((y * 4 + x) * 4 + zl) * 4 + zh) * 2 + c


def weight_pairs(shift):
    pairs = []
    for y in range(4):
        for x in range(4):
            for zl in range(4):
                for zh in range(4):
                    for c in range(2):
                        target = place(zh, 2 * c + x % 2, (zl + shift) % 4, y, x // 2)
                        pairs.append((place(y, x, zl, zh, c), target))
    return pairs


def rotate(values, axis, shift):
    return lax.ppermute(values, axis, [(i, (i + shift) % 4) for i in range(4)])


def swap(values):
    return lax.ppermute(values, "c", [(0, 1), (1, 0)])


def take(values, index):
    return lax.dynamic_index_in_dim(values, index.astype(jnp.uint32), 0, False)


def local(q_feat, k_feat, v_feat, stream, filters, w_out):
    zl, zh, c = lax.axis_index("zl"), lax.axis_index("zh"), lax.axis_index("c")
    mixed = (k_feat.astype(jnp.float32) * v_feat.astype(jnp.float32)).astype(jnp.bfloat16)
    sent = lax.all_to_all(mixed.T.reshape(N, 8, B), SEQ, 0, 0, tiled=True)

    block = w_out.T
    pieces = jnp.stack([lax.ppermute(block, ALL, weight_pairs(s)) for s in range(4)])
    order = jnp.stack([take(pieces, (zl - i) & 3) for i in range(4)])
    weights = lax.all_gather(order, ("y", "x"), axis=0, tiled=True).reshape(8, 512, 512)

    conv = causal_conv(sent.transpose(1, 0, 2), filters).transpose(1, 0, 2)
    conv = lax.all_to_all(conv, SEQ, 0, 0, tiled=True).reshape(512, B)
    gated = (q_feat.T.astype(jnp.float32) * conv.astype(jnp.float32)).astype(jnp.bfloat16)

    total = stream.astype(jnp.float32)
    for shift in (0, 1, -1, 2):
        mine = gated if shift == 0 else rotate(gated, "zh", shift)
        for core, part in ((c, mine), (1 - c, swap(mine))):
            rows = take(weights, 2 * ((zh - shift) & 3) + core)
            total = total + lax.dot_general(
                part, rows, (((0,), (1,)), ((), ())), preferred_element_type=jnp.float32
            )
    return total.astype(jnp.bfloat16)


def solution(mesh):
    fine = Mesh(np.asarray(mesh.devices).reshape(4, 4, 4, 4, 2), ALL)
    tp = ("zh", "c")

    def run(*args):
        with jax.sharding.use_abstract_mesh(fine.abstract_mesh):
            return jax.shard_map(
                local,
                mesh=fine,
                in_specs=(P(SEQ, tp),) * 4 + (P(tp + SEQ, None), P(tp, SEQ)),
                out_specs=P(SEQ, tp),
                check_vma=False,
            )(*args)

    return run
```

```python
import functools

import jax
import jax.numpy as jnp
import numpy as np
from jax import lax
from jax.experimental import pallas as pl
from jax.experimental.pallas import tpu as pltpu
from jax.sharding import Mesh
from jax.sharding import PartitionSpec as P


SEQ = ("y", "x", "zl")
ALL = ("y", "x", "zl", "zh", "c")
B = 256
N = 64
TOP = B * (N - 1) + 128
ROWS = TOP + B


def build_bank(h_ref, c, bank):
    lane = lax.broadcasted_iota(jnp.int32, (16, 128), 1)
    row = lax.broadcasted_iota(jnp.int32, (16, 128), 0)
    low = lane < row
    zero = jnp.zeros((16, 128), jnp.bfloat16)

    def put(w, val):
        v = TOP // 16 - w
        if 0 <= v < ROWS // 16:
            bank[pl.ds(16 * v, 16), :] = val

    rolled_before = jnp.zeros((16, 128), jnp.float32)
    before = zero
    for w in range(-16, -8):
        put(w, zero)
    for m in range(128):
        taps = jnp.broadcast_to(h_ref[c, pl.ds(m, 1), :], (16, 128))
        rolled = pltpu.roll(taps, 0, 1, stride=1, stride_axis=0)
        here = jnp.where(low, rolled_before, rolled).astype(jnp.bfloat16)
        rolled_before = rolled
        for j in range(1, 8):
            put(8 * (m - 1) + j, jnp.concatenate([before[:, 16 * j :], here[:, : 16 * j]], axis=1))
        put(8 * m, here)
        before = here


def conv_body(x_ref, h_ref, o_ref, padded, bank, acc0, acc1):
    padded[pl.ds(0, N), :] = jnp.zeros((N, B), jnp.float32)

    def channel(c, carry):
        padded[pl.ds(N, N), :] = x_ref[c].astype(jnp.float32)
        build_bank(h_ref, c, bank)
        for k in range(N):
            mxu, stage = k % 2, (k // 2) % 2
            r0 = TOP - B * k
            rhs = jnp.concatenate([bank[pl.ds(r0, B), :], bank[pl.ds(r0 - 128, B), :]], axis=1)
            pltpu.matmul_push_rhs(rhs, stage, mxu)
            lhs = padded[pl.ds(N - k, N), :].astype(jnp.bfloat16)
            pltpu.matmul_acc_lhs((acc0, acc1)[mxu], lhs, load_staged_rhs=stage)
        o_ref[c] = (pltpu.matmul_pop(acc0) + pltpu.matmul_pop(acc1)).astype(jnp.bfloat16)
        return carry

    lax.fori_loop(0, 8, channel, 0)


def conv_kernel(*refs):
    pl.run_scoped(
        functools.partial(conv_body, *refs),
        pltpu.ACC(0)((N, B), jnp.float32),
        pltpu.ACC(1)((N, B), jnp.float32),
    )


def causal_conv(x, taps):
    return pl.pallas_call(
        conv_kernel,
        out_shape=jax.ShapeDtypeStruct((8, N, B), jnp.bfloat16),
        in_specs=[pl.BlockSpec(memory_space=pltpu.VMEM)] * 2,
        out_specs=pl.BlockSpec(memory_space=pltpu.VMEM),
        scratch_shapes=[
            pltpu.VMEM((2 * N, B), jnp.float32),
            pltpu.VMEM((ROWS, 128), jnp.bfloat16),
        ],
        cost_estimate=pl.CostEstimate(flops=2**32, bytes_accessed=2**20, transcendentals=0),
        name="causal_conv",
    )(x, taps.reshape(8, 128, 128))


def mix_kernel(k_ref, v_ref, o_ref):
    mixed = k_ref[...].astype(jnp.float32) * v_ref[...].astype(jnp.float32)
    o_ref[...] = mixed.astype(jnp.bfloat16).T


def turn_kernel(q_ref, o_ref):
    o_ref[...] = q_ref[...].T


def small(kernel, *args):
    return pl.pallas_call(
        kernel,
        out_shape=jax.ShapeDtypeStruct((512, B), jnp.bfloat16),
        in_specs=[pl.BlockSpec(memory_space=pltpu.VMEM)] * len(args),
        out_specs=pl.BlockSpec(memory_space=pltpu.VMEM),
        cost_estimate=pl.CostEstimate(flops=2**18, bytes_accessed=2**19, transcendentals=0),
    )(*args)


def place(y, x, zl, zh, c):
    return (((y * 4 + x) * 4 + zl) * 4 + zh) * 2 + c


def weight_pairs():
    pairs = []
    for y in range(4):
        for x in range(4):
            for zl in range(4):
                for zh in range(4):
                    for c in range(2):
                        target = place(zh, 2 * c + x % 2, zl, y, x // 2)
                        pairs.append((place(y, x, zl, zh, c), target))
    return pairs


def rotate(values, axis, shift):
    return lax.ppermute(values, axis, [(i, (i + shift) % 4) for i in range(4)])


def swap(values):
    return lax.ppermute(values, "c", [(0, 1), (1, 0)])


def take(values, index):
    return lax.dynamic_index_in_dim(values, index.astype(jnp.uint32), 0, False)


def step(q_feat, k_feat, v_feat, stream, filters, w_out):
    y, zh, c = lax.axis_index("y"), lax.axis_index("zh"), lax.axis_index("c")
    mixed = small(mix_kernel, k_feat, v_feat).reshape(N, 8, B)
    sent = lax.all_to_all(mixed, SEQ, 0, 0, tiled=True)

    block = lax.ppermute(w_out.T, ALL, weight_pairs())
    block = jnp.broadcast_to(block[None], (16, 64, 512))
    row = lax.all_to_all(block, ("x", "zl"), 0, 0, tiled=True)
    row = row.reshape(2, 512, 512)
    weights = [row]
    for s in (1, -1, 2):
        weights.append(rotate(row, "y", s))

    conv = causal_conv(sent.transpose(1, 0, 2), filters)
    conv = conv.transpose(1, 0, 2)
    conv = lax.all_to_all(conv, SEQ, 0, 0, tiled=True).reshape(512, B)
    q_rows = small(turn_kernel, q_feat)
    gated = (q_rows.astype(jnp.float32) * conv.astype(jnp.float32)).astype(jnp.bfloat16)

    after = rotate(gated, "zh", 1)
    before = rotate(gated, "zh", -1)
    far_low = rotate(after[:256], "zh", 1)
    far_high = rotate(before[256:], "zh", -1)
    far = jnp.concatenate([far_low, far_high], axis=0)
    mine = jnp.stack([gated, after, far, before])
    other = jnp.stack([swap(p) for p in (gated, after, far, before)])

    total = stream.astype(jnp.float32)
    for shift, rows in zip((0, 1, -1, 2), weights):
        where = (zh - y + shift) & 3
        pair = take(mine, where), take(other, where)
        for core in range(2):
            part = jnp.where(c == core, *pair)
            total = total + lax.dot_general(
                part, rows[core], (((0,), (1,)), ((), ())), preferred_element_type=jnp.float32
            )
    return total.astype(jnp.bfloat16)


def solution(mesh):
    fine = Mesh(np.asarray(mesh.devices).reshape(4, 4, 4, 4, 2), ALL)
    tp = ("zh", "c")

    def run(*args):
        with jax.sharding.use_abstract_mesh(fine.abstract_mesh):
            return jax.shard_map(
                step,
                mesh=fine,
                in_specs=(P(SEQ, tp),) * 4 + (P(tp + SEQ, None), P(tp, SEQ)),
                out_specs=P(SEQ, tp),
                check_vma=False,
            )(*args)

    return run
```

```python
import functools

import jax
import jax.numpy as jnp
import numpy as np
from jax import lax
from jax.experimental import pallas as pl
from jax.experimental.pallas import tpu as pltpu
from jax.sharding import Mesh
from jax.sharding import PartitionSpec as P


SEQ = ("y", "x", "zl")
ALL = ("y", "x", "zl", "zh", "c")
B = 256
N = 64


def prep_kernel(h_ref, o_ref, ws):
    row = lax.broadcasted_iota(jnp.int32, (16, 256), 0)
    chunk = lax.broadcasted_iota(jnp.int32, (16, 256), 1) // 16
    lane8 = lax.broadcasted_iota(jnp.int32, (8, 128), 1)
    row8 = lax.broadcasted_iota(jnp.int32, (8, 128), 0)
    low = lane8 < 16 * (row8 + 1)

    def channel(c, carry):
        for j in range(4):
            x = h_ref[c, pl.ds(16 * j, 16), :]
            for k in range(4):
                n = 2**k
                rows, chunks = (row & n) == 0, (chunk & n) == 0
                up, down = pltpu.roll(x, 16 - n, 0), pltpu.roll(x, n, 0)
                right, left = pltpu.roll(x, 16 * n, 1), pltpu.roll(x, 256 - 16 * n, 1)
                x = jnp.where(rows, jnp.where(chunks, up, right), jnp.where(chunks, left, down))
            ws[:, pl.ds(256 * (3 - j), 256)] = x
        zero = jnp.zeros((8, 128), jnp.float32)
        for g in range(16):
            rolled = []
            for m in range(8):
                t = jnp.broadcast_to(ws[pl.ds(g, 1), pl.ds(128 * m, 128)], (8, 128))
                rolled.append(pltpu.roll(t, 16, 1, stride=16, stride_axis=0))
            rolled += [zero, zero]
            q = [None] + [jnp.where(low, rolled[m - 1], rolled[m]) for m in range(1, 10)]
            p = {m: jnp.concatenate([q[m], q[m - 1]], axis=0).astype(jnp.bfloat16) for m in range(2, 10)}
            for d in range(4):
                o_ref[c, d, g] = jnp.concatenate([p[8 - 2 * d], p[9 - 2 * d]], axis=1)
        return carry

    lax.fori_loop(0, 8, channel, 0)


def prep(h):
    return pl.pallas_call(
        prep_kernel,
        out_shape=jax.ShapeDtypeStruct((8, 4, 16, 16, 256), jnp.bfloat16),
        in_specs=[pl.BlockSpec(memory_space=pltpu.VMEM)],
        out_specs=pl.BlockSpec(memory_space=pltpu.VMEM),
        scratch_shapes=[pltpu.VMEM((16, 1024), jnp.float32)],
        cost_estimate=pl.CostEstimate(flops=2**26, bytes_accessed=2**22, transcendentals=0),
        name="prep",
    )(h.reshape(8, N, B))


def conv_body(x_ref, p_ref, o_ref, xs, gx, next_even, next_odd, *accs):
    xs[...] = x_ref[...].astype(jnp.float32)
    lane = lax.broadcasted_iota(jnp.int32, (16, 128), 1)
    row = lax.broadcasted_iota(jnp.int32, (16, 128), 0)
    low = lane < row
    next_even[...] = jnp.zeros_like(next_even)
    next_odd[...] = jnp.zeros_like(next_odd)
    for c in range(8):
        slot = gx[c % 2]
        before = jnp.zeros((16, 128), jnp.float32)
        for t in range(128):
            b, half = t // 2, t % 2
            tokens = jnp.broadcast_to(xs[b, pl.ds(c, 1), pl.ds(128 * half, 128)], (16, 128))
            rolled = pltpu.roll(tokens, 0, 1, stride=1, stride_axis=0)
            slot[b, :, pl.ds(128 * half, 128)] = jnp.where(low, before, rolled).astype(jnp.bfloat16)
            before = rolled
        for kt in range(4):
            rhs = slot[pl.ds(16 * kt, 16)].reshape(256, 256)
            for u in range(2):
                pltpu.matmul_push_rhs(rhs, kt % 2, u)
            for a in range(kt, 4):
                for u in range(2):
                    lhs = p_ref[c, a - kt, pl.ds(8 * u, 8)].reshape(128, 256)
                    pltpu.matmul_acc_lhs(accs[2 * a + u], lhs, load_staged_rhs=kt % 2 if a == kt else None)
        even, odd = [], []
        for a in range(4):
            z0, z1 = pltpu.matmul_pop(accs[2 * a]), pltpu.matmul_pop(accs[2 * a + 1])
            s = [None] * 4
            for g in range(8):
                e = z0[16 * g : 16 * g + 16, :128]
                o = z0[16 * g : 16 * g + 16, 128:] + z1[16 * g : 16 * g + 16, :128]
                n = z1[16 * g : 16 * g + 16, 128:]
                if g == 0:
                    s = [e, o, n, None]
                    continue
                e, o, n = (pltpu.roll(v, 16 * g, 1) for v in (e, o, n))
                mask = lane < 16 * g
                s[0] = s[0] + jnp.where(mask, 0.0, e)
                s[1] = s[1] + jnp.where(mask, e, o)
                s[2] = s[2] + jnp.where(mask, o, n)
                last = jnp.where(mask, n, 0.0)
                s[3] = last if s[3] is None else s[3] + last
            even.append(s[0])
            odd.append(s[1])
            next_even[pl.ds(16 * a + 1, 16), :] = s[2]
            next_odd[pl.ds(16 * a + 1, 16), :] = s[3]
        for a in range(4):
            rows = pl.ds(16 * a, 16)
            xs[rows, c, pl.ds(0, 128)] = even[a] + next_even[rows, :]
            xs[rows, c, pl.ds(128, 128)] = odd[a] + next_odd[rows, :]
    o_ref[...] = xs[...].astype(jnp.bfloat16)


def conv_kernel(*refs):
    pl.run_scoped(functools.partial(wrap, refs), *[pltpu.ACC(u)((128, B), jnp.float32) for _ in range(4) for u in range(2)])


def wrap(refs, *accs):
    x_ref, p_ref, o_ref, xs, g0, g1, ne, no = refs
    conv_body(x_ref, p_ref, o_ref, xs, (g0, g1), ne, no, *accs)


def causal_conv(x, p):
    return pl.pallas_call(
        conv_kernel,
        out_shape=jax.ShapeDtypeStruct((N, 8, B), jnp.bfloat16),
        in_specs=[pl.BlockSpec(memory_space=pltpu.VMEM)] * 2,
        out_specs=pl.BlockSpec(memory_space=pltpu.VMEM),
        scratch_shapes=[
            pltpu.VMEM((N, 8, B), jnp.float32),
            pltpu.VMEM((N, 16, B), jnp.bfloat16),
            pltpu.VMEM((N, 16, B), jnp.bfloat16),
            pltpu.VMEM((N + 8, 128), jnp.float32),
            pltpu.VMEM((N + 8, 128), jnp.float32),
        ],
        cost_estimate=pl.CostEstimate(flops=2**32, bytes_accessed=2**22, transcendentals=0),
        name="causal_conv",
    )(x, p)


def mix_kernel(k_ref, v_ref, o_ref):
    mixed = k_ref[...].astype(jnp.float32) * v_ref[...].astype(jnp.float32)
    o_ref[...] = mixed.astype(jnp.bfloat16).T


def turn_kernel(q_ref, o_ref):
    o_ref[...] = q_ref[...].T


def small(kernel, *args):
    return pl.pallas_call(
        kernel,
        out_shape=jax.ShapeDtypeStruct((512, B), jnp.bfloat16),
        in_specs=[pl.BlockSpec(memory_space=pltpu.VMEM)] * len(args),
        out_specs=pl.BlockSpec(memory_space=pltpu.VMEM),
        cost_estimate=pl.CostEstimate(flops=2**18, bytes_accessed=2**19, transcendentals=0),
    )(*args)


def place(y, x, zl, zh, c):
    return (((y * 4 + x) * 4 + zl) * 4 + zh) * 2 + c


def weight_pairs():
    pairs = []
    for y in range(4):
        for x in range(4):
            for zl in range(4):
                for zh in range(4):
                    for c in range(2):
                        target = place(zh, 2 * c + x % 2, zl, y, x // 2)
                        pairs.append((place(y, x, zl, zh, c), target))
    return pairs


def rotate(values, axis, shift):
    return lax.ppermute(values, axis, [(i, (i + shift) % 4) for i in range(4)])


def swap(values):
    return lax.ppermute(values, "c", [(0, 1), (1, 0)])


def take(values, index):
    return lax.dynamic_index_in_dim(values, index.astype(jnp.uint32), 0, False)


def step(q_feat, k_feat, v_feat, stream, filters, w_out):
    y, zh, c = lax.axis_index("y"), lax.axis_index("zh"), lax.axis_index("c")
    mixed = small(mix_kernel, k_feat, v_feat).reshape(N, 8, B)
    sent = lax.all_to_all(mixed, SEQ, 0, 0, tiled=True)

    block = lax.ppermute(w_out.T, ALL, weight_pairs())
    block = jnp.broadcast_to(block[None], (16, 64, 512))
    row = lax.all_to_all(block, ("x", "zl"), 0, 0, tiled=True)
    row = row.reshape(2, 512, 512)
    weights = [row]
    for s in (1, -1, 2):
        weights.append(rotate(row, "y", s))

    taps = prep(filters)
    conv = causal_conv(sent, taps)
    conv = lax.all_to_all(conv, SEQ, 0, 0, tiled=True).reshape(512, B)
    q_rows = small(turn_kernel, q_feat)
    gated = (q_rows.astype(jnp.float32) * conv.astype(jnp.float32)).astype(jnp.bfloat16)

    after = rotate(gated, "zh", 1)
    before = rotate(gated, "zh", -1)
    far_low = rotate(after[:256], "zh", 1)
    far_high = rotate(before[256:], "zh", -1)
    far = jnp.concatenate([far_low, far_high], axis=0)
    mine = jnp.stack([gated, after, far, before])
    other = jnp.stack([swap(p) for p in (gated, after, far, before)])

    total = stream.astype(jnp.float32)
    for shift, rows in zip((0, 1, -1, 2), weights):
        where = (zh - y + shift) & 3
        pair = take(mine, where), take(other, where)
        for core in range(2):
            part = jnp.where(c == core, *pair)
            total = total + lax.dot_general(
                part, rows[core], (((0,), (1,)), ((), ())), preferred_element_type=jnp.float32
            )
    return total.astype(jnp.bfloat16)


def solution(mesh):
    fine = Mesh(np.asarray(mesh.devices).reshape(4, 4, 4, 4, 2), ALL)
    tp = ("zh", "c")

    def run(*args):
        with jax.sharding.use_abstract_mesh(fine.abstract_mesh):
            return jax.shard_map(
                step,
                mesh=fine,
                in_specs=(P(SEQ, tp),) * 4 + (P(tp + SEQ, None), P(tp, SEQ)),
                out_specs=P(SEQ, tp),
                check_vma=False,
            )(*args)

    return run
```

```python
import functools

import jax
import jax.numpy as jnp
import numpy as np
from jax import lax
from jax.experimental import pallas as pl
from jax.experimental.pallas import tpu as pltpu
from jax.sharding import Mesh
from jax.sharding import PartitionSpec as P


SEQ = ("y", "x", "zl")
ALL = ("y", "x", "zl", "zh", "c")
B = 256
N = 64


def prep_kernel(h_ref, o_ref, ws):
    row = lax.broadcasted_iota(jnp.int32, (16, 256), 0)
    chunk = lax.broadcasted_iota(jnp.int32, (16, 256), 1) // 16
    lane8 = lax.broadcasted_iota(jnp.int32, (8, 128), 1)
    row8 = lax.broadcasted_iota(jnp.int32, (8, 128), 0)
    low = lane8 < 16 * (row8 + 1)

    def channel(c, carry):
        for j in range(4):
            x = h_ref[c, pl.ds(16 * j, 16), :]
            for k in range(4):
                n = 2**k
                rows, chunks = (row & n) == 0, (chunk & n) == 0
                up, down = pltpu.roll(x, 16 - n, 0), pltpu.roll(x, n, 0)
                right, left = pltpu.roll(x, 16 * n, 1), pltpu.roll(x, 256 - 16 * n, 1)
                x = jnp.where(rows, jnp.where(chunks, up, right), jnp.where(chunks, left, down))
            ws[:, pl.ds(256 * (3 - j), 256)] = x
        zero = jnp.zeros((8, 128), jnp.float32)
        for g in range(16):
            rolled = []
            for m in range(8):
                t = jnp.broadcast_to(ws[pl.ds(g, 1), pl.ds(128 * m, 128)], (8, 128))
                rolled.append(pltpu.roll(t, 16, 1, stride=16, stride_axis=0))
            rolled += [zero, zero]
            q = [None] + [jnp.where(low, rolled[m - 1], rolled[m]) for m in range(1, 10)]
            p = {m: jnp.concatenate([q[m], q[m - 1]], axis=0).astype(jnp.bfloat16) for m in range(2, 10)}
            for d in range(4):
                o_ref[c, d, g] = jnp.concatenate([p[8 - 2 * d], p[9 - 2 * d]], axis=1)
        return carry

    lax.fori_loop(0, 8, channel, 0)


def prep(h):
    return pl.pallas_call(
        prep_kernel,
        out_shape=jax.ShapeDtypeStruct((8, 4, 16, 16, 256), jnp.bfloat16),
        in_specs=[pl.BlockSpec(memory_space=pltpu.VMEM)],
        out_specs=pl.BlockSpec(memory_space=pltpu.VMEM),
        scratch_shapes=[pltpu.VMEM((16, 1024), jnp.float32)],
        cost_estimate=pl.CostEstimate(flops=2**26, bytes_accessed=2**22, transcendentals=0),
        name="prep",
    )(h.reshape(8, N, B))


def conv_body(x_ref, p_ref, o_ref, xs, gx, next_even, next_odd, *accs):
    xs[...] = x_ref[...].astype(jnp.float32)
    lane = lax.broadcasted_iota(jnp.int32, (16, 128), 1)
    row = lax.broadcasted_iota(jnp.int32, (16, 128), 0)
    low = lane < row
    next_even[...] = jnp.zeros_like(next_even)
    next_odd[...] = jnp.zeros_like(next_odd)
    for c in range(8):
        slot = gx[c % 2]
        before = jnp.zeros((16, 128), jnp.float32)
        for t in range(128):
            b, half = t // 2, t % 2
            tokens = jnp.broadcast_to(xs[b, pl.ds(c, 1), pl.ds(128 * half, 128)], (16, 128))
            rolled = pltpu.roll(tokens, 0, 1, stride=1, stride_axis=0)
            slot[b, :, pl.ds(128 * half, 128)] = jnp.where(low, before, rolled).astype(jnp.bfloat16)
            before = rolled
        for kt in range(4):
            rhs = slot[pl.ds(16 * kt, 16)].reshape(256, 256)
            for u in range(2):
                pltpu.matmul_push_rhs(rhs, kt % 2, u)
            for a in range(kt, 4):
                for u in range(2):
                    lhs = p_ref[c, a - kt, pl.ds(8 * u, 8)].reshape(128, 256)
                    pltpu.matmul_acc_lhs(accs[2 * a + u], lhs, load_staged_rhs=kt % 2 if a == kt else None)
        even, odd = [], []
        for a in range(4):
            z0, z1 = pltpu.matmul_pop(accs[2 * a]), pltpu.matmul_pop(accs[2 * a + 1])
            s = [None] * 4
            for g in range(8):
                e = z0[16 * g : 16 * g + 16, :128]
                o = z0[16 * g : 16 * g + 16, 128:] + z1[16 * g : 16 * g + 16, :128]
                n = z1[16 * g : 16 * g + 16, 128:]
                if g == 0:
                    s = [e, o, n, None]
                    continue
                e, o, n = (pltpu.roll(v, 16 * g, 1) for v in (e, o, n))
                mask = lane < 16 * g
                s[0] = s[0] + jnp.where(mask, 0.0, e)
                s[1] = s[1] + jnp.where(mask, e, o)
                s[2] = s[2] + jnp.where(mask, o, n)
                last = jnp.where(mask, n, 0.0)
                s[3] = last if s[3] is None else s[3] + last
            even.append(s[0])
            odd.append(s[1])
            next_even[pl.ds(16 * a + 1, 16), :] = s[2]
            next_odd[pl.ds(16 * a + 1, 16), :] = s[3]
        for a in range(4):
            rows = pl.ds(16 * a, 16)
            xs[rows, c, pl.ds(0, 128)] = even[a] + next_even[rows, :]
            xs[rows, c, pl.ds(128, 128)] = odd[a] + next_odd[rows, :]
    o_ref[...] = xs[...].astype(jnp.bfloat16)


def conv_kernel(*refs):
    pl.run_scoped(functools.partial(wrap, refs), *[pltpu.ACC(u)((128, B), jnp.float32) for _ in range(4) for u in range(2)])


def wrap(refs, *accs):
    x_ref, p_ref, o_ref, xs, g0, g1, ne, no = refs
    conv_body(x_ref, p_ref, o_ref, xs, (g0, g1), ne, no, *accs)


def causal_conv(x, p):
    return pl.pallas_call(
        conv_kernel,
        out_shape=jax.ShapeDtypeStruct((N, 8, B), jnp.bfloat16),
        in_specs=[pl.BlockSpec(memory_space=pltpu.VMEM)] * 2,
        out_specs=pl.BlockSpec(memory_space=pltpu.VMEM),
        scratch_shapes=[
            pltpu.VMEM((N, 8, B), jnp.float32),
            pltpu.VMEM((N, 16, B), jnp.bfloat16),
            pltpu.VMEM((N, 16, B), jnp.bfloat16),
            pltpu.VMEM((N + 8, 128), jnp.float32),
            pltpu.VMEM((N + 8, 128), jnp.float32),
        ],
        cost_estimate=pl.CostEstimate(flops=2**32, bytes_accessed=2**22, transcendentals=0),
        name="causal_conv",
    )(x, p)


def mix_kernel(k_ref, v_ref, o_ref):
    mixed = k_ref[...].astype(jnp.float32) * v_ref[...].astype(jnp.float32)
    o_ref[...] = mixed.astype(jnp.bfloat16).T


def turn_kernel(q_ref, o_ref):
    o_ref[...] = q_ref[...].T


def small(kernel, *args):
    return pl.pallas_call(
        kernel,
        out_shape=jax.ShapeDtypeStruct((512, B), jnp.bfloat16),
        in_specs=[pl.BlockSpec(memory_space=pltpu.VMEM)] * len(args),
        out_specs=pl.BlockSpec(memory_space=pltpu.VMEM),
        cost_estimate=pl.CostEstimate(flops=2**18, bytes_accessed=2**19, transcendentals=0),
    )(*args)


def place(y, x, zl, zh, c):
    return (((y * 4 + x) * 4 + zl) * 4 + zh) * 2 + c


def weight_pairs():
    pairs = []
    for y in range(4):
        for x in range(4):
            for zl in range(4):
                for zh in range(4):
                    for c in range(2):
                        target = place(zh, 2 * c + x % 2, zl, y, x // 2)
                        pairs.append((place(y, x, zl, zh, c), target))
    return pairs


def rotate(values, axis, shift):
    return lax.ppermute(values, axis, [(i, (i + shift) % 4) for i in range(4)])


def swap(values):
    return lax.ppermute(values, "c", [(0, 1), (1, 0)])


def take(values, index):
    return lax.dynamic_index_in_dim(values, index.astype(jnp.uint32), 0, False)


def step(q_feat, k_feat, v_feat, stream, filters, w_out):
    y, zh, c = lax.axis_index("y"), lax.axis_index("zh"), lax.axis_index("c")
    mixed = small(mix_kernel, k_feat, v_feat).reshape(N, 8, B)
    sent = lax.all_to_all(mixed, SEQ, 0, 0, tiled=True)

    block = lax.ppermute(w_out.T, ALL, weight_pairs())

    def gathered(part, axis):
        pieces = [part]
        for s in (1, 2, 3):
            pieces.append(rotate(part, axis, s))
        pieces, here = jnp.stack(pieces), lax.axis_index(axis)
        return jnp.stack([take(pieces, (here - i) & 3) for i in range(4)])

    row = gathered(block, "zl").reshape(256, 512)
    row = gathered(row, "x").reshape(2, 512, 512)
    weights = [row]
    for s in (1, -1, 2):
        weights.append(rotate(row, "y", s))

    taps = prep(filters)
    conv = causal_conv(sent, taps)
    conv = lax.all_to_all(conv, SEQ, 0, 0, tiled=True).reshape(512, B)
    q_rows = small(turn_kernel, q_feat)
    gated = (q_rows.astype(jnp.float32) * conv.astype(jnp.float32)).astype(jnp.bfloat16)

    after = rotate(gated, "zh", 1)
    before = rotate(gated, "zh", -1)
    far_low = rotate(after[:256], "zh", 1)
    far_high = rotate(before[256:], "zh", -1)
    far = jnp.concatenate([far_low, far_high], axis=0)
    mine = jnp.stack([gated, after, far, before])
    other = jnp.stack([swap(p) for p in (gated, after, far, before)])

    total = stream.astype(jnp.float32)
    for shift, rows in zip((0, 1, -1, 2), weights):
        where = (zh - y + shift) & 3
        pair = take(mine, where), take(other, where)
        for core in range(2):
            part = jnp.where(c == core, *pair)
            total = total + lax.dot_general(
                part, rows[core], (((0,), (1,)), ((), ())), preferred_element_type=jnp.float32
            )
    return total.astype(jnp.bfloat16)


def solution(mesh):
    fine = Mesh(np.asarray(mesh.devices).reshape(4, 4, 4, 4, 2), ALL)
    tp = ("zh", "c")

    def run(*args):
        with jax.sharding.use_abstract_mesh(fine.abstract_mesh):
            return jax.shard_map(
                step,
                mesh=fine,
                in_specs=(P(SEQ, tp),) * 4 + (P(tp + SEQ, None), P(tp, SEQ)),
                out_specs=P(SEQ, tp),
                check_vma=False,
            )(*args)

    return run
```

```python
import functools

import jax
import jax.numpy as jnp
import numpy as np
from jax import lax
from jax.experimental import pallas as pl
from jax.experimental.pallas import tpu as pltpu
from jax.sharding import Mesh
from jax.sharding import PartitionSpec as P


SEQ = ("y", "x", "zl")
ALL = ("y", "x", "zl", "zh", "c")
B = 256
N = 64


def prep_kernel(h_ref, o_ref, ws):
    row = lax.broadcasted_iota(jnp.int32, (16, 256), 0)
    chunk = lax.broadcasted_iota(jnp.int32, (16, 256), 1) // 16
    lane8 = lax.broadcasted_iota(jnp.int32, (8, 128), 1)
    row8 = lax.broadcasted_iota(jnp.int32, (8, 128), 0)
    low = lane8 < 16 * (row8 + 1)

    def channel(c, carry):
        for j in range(4):
            halves = [h_ref[c, pl.ds(32 * j + n, 16, stride=2), :] for n in range(2)]
            x = jnp.concatenate(halves, axis=1)
            for k in range(4):
                n = 2**k
                rows, chunks = (row & n) == 0, (chunk & n) == 0
                up, down = pltpu.roll(x, 16 - n, 0), pltpu.roll(x, n, 0)
                right, left = pltpu.roll(x, 16 * n, 1), pltpu.roll(x, 256 - 16 * n, 1)
                x = jnp.where(rows, jnp.where(chunks, up, right), jnp.where(chunks, left, down))
            ws[:, pl.ds(256 * (3 - j), 256)] = x
        zero = jnp.zeros((8, 128), jnp.float32)
        for g in range(16):
            rolled = []
            for m in range(8):
                t = jnp.broadcast_to(ws[pl.ds(g, 1), pl.ds(128 * m, 128)], (8, 128))
                rolled.append(pltpu.roll(t, 16, 1, stride=16, stride_axis=0))
            rolled += [zero, zero]
            q = [None] + [jnp.where(low, rolled[m - 1], rolled[m]) for m in range(1, 10)]
            p = {m: jnp.concatenate([q[m], q[m - 1]], axis=0).astype(jnp.bfloat16) for m in range(2, 10)}
            for d in range(4):
                o_ref[c, d, g] = jnp.concatenate([p[8 - 2 * d], p[9 - 2 * d]], axis=1)
        return carry

    lax.fori_loop(0, 8, channel, 0)


def prep(h):
    return pl.pallas_call(
        prep_kernel,
        out_shape=jax.ShapeDtypeStruct((8, 4, 16, 16, 256), jnp.bfloat16),
        in_specs=[pl.BlockSpec(memory_space=pltpu.VMEM)],
        out_specs=pl.BlockSpec(memory_space=pltpu.VMEM),
        scratch_shapes=[pltpu.VMEM((16, 1024), jnp.float32)],
        cost_estimate=pl.CostEstimate(flops=2**26, bytes_accessed=2**22, transcendentals=0),
        name="prep",
    )(h.reshape(8, 2 * N, 128))


def conv_body(x_ref, p_ref, o_ref, xs, gx, next_even, next_odd, *accs):
    xs[...] = x_ref[...].astype(jnp.float32)
    lane = lax.broadcasted_iota(jnp.int32, (16, 128), 1)
    row = lax.broadcasted_iota(jnp.int32, (16, 128), 0)
    low = lane < row
    next_even[...] = jnp.zeros_like(next_even)
    next_odd[...] = jnp.zeros_like(next_odd)
    for c in range(8):
        slot = gx[c % 2]
        before = jnp.zeros((16, 128), jnp.float32)
        for t in range(128):
            b, half = t // 2, t % 2
            tokens = jnp.broadcast_to(xs[b, pl.ds(c, 1), pl.ds(128 * half, 128)], (16, 128))
            rolled = pltpu.roll(tokens, 0, 1, stride=1, stride_axis=0)
            slot[b, :, pl.ds(128 * half, 128)] = jnp.where(low, before, rolled).astype(jnp.bfloat16)
            before = rolled
        for kt in range(4):
            rhs = slot[pl.ds(16 * kt, 16)].reshape(256, 256)
            for u in range(2):
                pltpu.matmul_push_rhs(rhs, kt % 2, u)
            for a in range(kt, 4):
                for u in range(2):
                    lhs = p_ref[c, a - kt, pl.ds(8 * u, 8)].reshape(128, 256)
                    pltpu.matmul_acc_lhs(accs[2 * a + u], lhs, load_staged_rhs=kt % 2 if a == kt else None)
        even, odd = [], []
        for a in range(4):
            z0, z1 = pltpu.matmul_pop(accs[2 * a]), pltpu.matmul_pop(accs[2 * a + 1])
            s = [None] * 4
            for g in range(8):
                e = z0[16 * g : 16 * g + 16, :128]
                o = z0[16 * g : 16 * g + 16, 128:] + z1[16 * g : 16 * g + 16, :128]
                n = z1[16 * g : 16 * g + 16, 128:]
                if g == 0:
                    s = [e, o, n, None]
                    continue
                e, o, n = (pltpu.roll(v, 16 * g, 1) for v in (e, o, n))
                mask = lane < 16 * g
                s[0] = s[0] + jnp.where(mask, 0.0, e)
                s[1] = s[1] + jnp.where(mask, e, o)
                s[2] = s[2] + jnp.where(mask, o, n)
                last = jnp.where(mask, n, 0.0)
                s[3] = last if s[3] is None else s[3] + last
            even.append(s[0])
            odd.append(s[1])
            next_even[pl.ds(16 * a + 1, 16), :] = s[2]
            next_odd[pl.ds(16 * a + 1, 16), :] = s[3]
        for a in range(4):
            rows = pl.ds(16 * a, 16)
            xs[rows, c, pl.ds(0, 128)] = even[a] + next_even[rows, :]
            xs[rows, c, pl.ds(128, 128)] = odd[a] + next_odd[rows, :]
    o_ref[...] = xs[...].astype(jnp.bfloat16)


def conv_kernel(*refs):
    pl.run_scoped(functools.partial(wrap, refs), *[pltpu.ACC(u)((128, B), jnp.float32) for _ in range(4) for u in range(2)])


def wrap(refs, *accs):
    x_ref, p_ref, o_ref, xs, g0, g1, ne, no = refs
    conv_body(x_ref, p_ref, o_ref, xs, (g0, g1), ne, no, *accs)


def causal_conv(x, p):
    return pl.pallas_call(
        conv_kernel,
        out_shape=jax.ShapeDtypeStruct((N, 8, B), jnp.bfloat16),
        in_specs=[pl.BlockSpec(memory_space=pltpu.VMEM)] * 2,
        out_specs=pl.BlockSpec(memory_space=pltpu.VMEM),
        scratch_shapes=[
            pltpu.VMEM((N, 8, B), jnp.float32),
            pltpu.VMEM((N, 16, B), jnp.bfloat16),
            pltpu.VMEM((N, 16, B), jnp.bfloat16),
            pltpu.VMEM((N + 8, 128), jnp.float32),
            pltpu.VMEM((N + 8, 128), jnp.float32),
        ],
        cost_estimate=pl.CostEstimate(flops=2**32, bytes_accessed=2**22, transcendentals=0),
        name="causal_conv",
    )(x, p)


def mix_kernel(k_ref, v_ref, o_ref):
    mixed = k_ref[...].astype(jnp.float32) * v_ref[...].astype(jnp.float32)
    o_ref[...] = mixed.astype(jnp.bfloat16).T


def turn_kernel(q_ref, o_ref):
    o_ref[...] = q_ref[...].T


def small(kernel, *args):
    return pl.pallas_call(
        kernel,
        out_shape=jax.ShapeDtypeStruct((512, B), jnp.bfloat16),
        in_specs=[pl.BlockSpec(memory_space=pltpu.VMEM)] * len(args),
        out_specs=pl.BlockSpec(memory_space=pltpu.VMEM),
        cost_estimate=pl.CostEstimate(flops=2**18, bytes_accessed=2**19, transcendentals=0),
    )(*args)


def place(y, x, zl, zh, c):
    return (((y * 4 + x) * 4 + zl) * 4 + zh) * 2 + c


def weight_pairs():
    pairs = []
    for y in range(4):
        for x in range(4):
            for zl in range(4):
                for zh in range(4):
                    for c in range(2):
                        target = place(zh, 2 * c + x % 2, zl, y, x // 2)
                        pairs.append((place(y, x, zl, zh, c), target))
    return pairs


def rotate(values, axis, shift):
    return lax.ppermute(values, axis, [(i, (i + shift) % 4) for i in range(4)])


def swap(values):
    return lax.ppermute(values, "c", [(0, 1), (1, 0)])


def take(values, index):
    return lax.dynamic_index_in_dim(values, index.astype(jnp.uint32), 0, False)


def step(q_feat, k_feat, v_feat, stream, filters, w_out):
    y, zh, c = lax.axis_index("y"), lax.axis_index("zh"), lax.axis_index("c")
    mixed = small(mix_kernel, k_feat, v_feat).reshape(N, 8, B)
    sent = lax.all_to_all(mixed, SEQ, 0, 0, tiled=True)

    block = lax.ppermute(w_out.T, ALL, weight_pairs())

    def gathered(part, axis):
        pieces = [part]
        for s in (1, 2, 3):
            pieces.append(rotate(part, axis, s))
        pieces, here = jnp.stack(pieces), lax.axis_index(axis)
        return jnp.stack([take(pieces, (here - i) & 3) for i in range(4)])

    row = gathered(block, "zl").reshape(256, 512)
    row = gathered(row, "x").reshape(2, 512, 512)
    weights = [row]
    for s in (1, 2, 3):
        weights.append(rotate(row, "y", s))

    taps = prep(filters)
    conv = causal_conv(sent, taps)
    conv = lax.all_to_all(conv, SEQ, 0, 0, tiled=True).reshape(512, B)
    q_rows = small(turn_kernel, q_feat)
    gated = (q_rows.astype(jnp.float32) * conv.astype(jnp.float32)).astype(jnp.bfloat16)

    after = rotate(gated, "zh", 1)
    before = rotate(gated, "zh", -1)
    far_low = rotate(after[:256], "zh", 1)
    far_high = rotate(before[256:], "zh", -1)
    weights = jnp.concatenate(weights, axis=0)

    def product(part, r, core, low=0):
        rows = take(weights, 2 * ((y - zh + r) & 3) + core)[:, low : low + part.shape[0]]
        return lax.dot_general(part, rows, (((0,), (1,)), ((), ())), preferred_element_type=jnp.float32)

    total = stream.astype(jnp.float32)
    for r, part in ((0, gated), (1, after), (3, before)):
        total = total + product(part, r, c)
        total = total + product(swap(part), r, 1 - c)
    for part, low in ((far_low, 0), (far_high, 256)):
        total = total + product(part, 2, c, low)
        total = total + product(swap(part), 2, 1 - c, low)
    return total.astype(jnp.bfloat16)


def solution(mesh):
    fine = Mesh(np.asarray(mesh.devices).reshape(4, 4, 4, 4, 2), ALL)
    tp = ("zh", "c")

    def run(*args):
        with jax.sharding.use_abstract_mesh(fine.abstract_mesh):
            return jax.shard_map(
                step,
                mesh=fine,
                in_specs=(P(SEQ, tp),) * 4 + (P(tp + SEQ, None), P(tp, SEQ)),
                out_specs=P(SEQ, tp),
                check_vma=False,
            )(*args)

    return run
```
